32 devices in a mesh: dom: 16 (over z, x, core), mem: 2 (over y).
Axes of the slice: x: 2, y: 2, z: 4, core: 2. Of those that a mesh axis runs over, the one named last changes fastest.
Arguments:
- ensemble: bfloat16 [12, 32, 65536], P('mem', None, 'dom'), may hold values from -6 to 6
- observed: float32 [32, 16384], P(None, 'dom'), may hold values from -6 to 6
- tile_weight: bfloat16 [1536, 128, 128], P('dom')
- tile_block: int32 [1536], P('dom'), may hold values from 0 to 31
- tile_target: int32 [1536], P('dom'), may hold values from 0 to 127, as said below
- tile_count: int32 [16], P('dom'), may hold values from 48 to 96, as said below
Outputs:
- crps: float32 [32, 16384], P(None, 'dom')
The draws below stay inside these ranges and needn't reach their ends.
Inputs may be any that keep to these rules, and one draw needn't show every extreme that they name: `tile_block`: a slot's source block, counted within its partition's cells. `tile_target`: slot k belongs to partition p = k // 96; its target tile is owned by one of the partitions p - 4 to p + 4, where partition o owns the 8 target tiles from o * 8 on. The live slots of partition p are the first tile_count[p] of its list; the rest are padding.
All inputs are finite; a program needn't handle non-finite values.
Results may differ from the reference program's by a relative error of at most 0.0003.
Values sent between devices are 32-bit elements; how exact they have to be, the bound alone decides.
A program may use at most 64 MiB of HBM per device.

```python
import math
import jax
import jax.numpy as jnp
from jax import lax

BLOCK = 128
REACH = 4
LEV = 32
SRC_DEV = 4096
TGT_DEV = 1024
TILES_DEV = 96
PARTITIONS = 16
MEMBERS = 12
SRC = 65536
TGT = 16384
TILES = 1536


def draw_tile_weight(key, part):
    key_diag, key_off = jax.random.split(key, 2)
    shape = (TILES, BLOCK, BLOCK)
    unit_diag = jnp.eye(BLOCK, dtype=jnp.float32)
    overall = (0.75 * TILES_DEV * BLOCK / TGT_DEV) ** (-0.5)
    diagonal = jax.random.uniform(key_diag, (TILES, 1, BLOCK), jnp.float32, 0.4, 1.2)
    rough = 0.03 * jax.random.normal(key_off, shape, jnp.float32)
    weights = (rough * (1.0 - unit_diag) + diagonal * unit_diag) * overall
    return weights.astype(jnp.bfloat16)


def draw_tile_target(key, part):
    partition = jnp.arange(TILES, dtype=jnp.int32) // TILES_DEV
    slot_place = jnp.arange(TILES, dtype=jnp.int32) % TILES_DEV
    lowest = jnp.maximum(partition - REACH, 0)
    highest = jnp.minimum(partition + REACH, PARTITIONS - 1)
    key_owner, key_tile = jax.random.split(key)
    owner = jax.random.randint(key_owner, (TILES,), lowest, highest + 1)
    owner = jnp.where(slot_place == 0, highest, owner)
    owner = jnp.where(slot_place == 1, lowest, owner)
    owned = TGT_DEV // BLOCK
    inner = jax.random.randint(key_tile, (TILES,), 0, owned)
    return (owner * owned + inner).astype(jnp.int32)


def draw_tile_count(key, part):
    key_count, key_full = jax.random.split(key)
    counts = jax.random.randint(key_count, (PARTITIONS,), TILES_DEV // 2, TILES_DEV + 1)
    fullest = jax.random.randint(key_full, (), 0, PARTITIONS)
    return jnp.where(jnp.arange(PARTITIONS, dtype=jnp.int32) == fullest, TILES_DEV, counts).astype(jnp.int32)


def set_ends(result, own_key, smallest, largest):
    longest = result.shape.index(max(result.shape))
    spots = []
    for shift in (0, 1):
        where = [jax.random.randint(jax.random.fold_in(own_key, axis), (), 0, length) for axis, length in enumerate(result.shape)]
        where[longest] = (where[longest] + shift) % result.shape[longest]
        spots.append(tuple(where))
    return result.at[spots[0]].set(smallest).at[spots[1]].set(largest)


def steps_of(own_key, shape, cuts, low, top_value):
    level = 1.0
    for axis_at, blocks in cuts:
        heights = jax.random.uniform(jax.random.fold_in(jax.random.fold_in(own_key, 6), axis_at), (blocks,), jnp.float32, low / len(cuts), top_value / len(cuts))
        level = level * jnp.repeat(jnp.exp(heights), shape[axis_at] // blocks).reshape((-1,) + (1,) * (len(shape) - 1 - axis_at))
    return level


def centred(own_key, dims, scale, limit, cuts=(), held_as=jnp.bfloat16):
    array = scale * jax.random.normal(own_key, dims, jnp.float32)
    if cuts:
        array = array * steps_of(own_key, dims, cuts, -0.22, 0.18)
    return jnp.clip(array, -limit, limit).astype(held_as)


def setup_inputs(seed: int = 0) -> dict:
    splits = jax.random.split(jax.random.key(seed), 7)
    ensemble = centred(splits[0], (MEMBERS, LEV, SRC), 1.0, 6.0, ((0, 2), (2, 16)))
    observed = centred(splits[1], (LEV, TGT), 1.0, 6.0, ((1, 16),), jnp.float32)
    tile_weight = draw_tile_weight(jax.random.fold_in(splits[6], 71), 0)
    tile_block = set_ends(jax.random.randint(splits[3], (TILES,), 0, SRC_DEV // BLOCK), jax.random.fold_in(splits[3], 1), 0, (SRC_DEV // BLOCK) - 1).astype(jnp.int32)
    tile_target = draw_tile_target(jax.random.fold_in(splits[6], 71), 0)
    tile_count = draw_tile_count(jax.random.fold_in(splits[6], 71), 0)
    return dict(ensemble=ensemble, observed=observed, tile_weight=tile_weight, tile_block=tile_block, tile_target=tile_target, tile_count=tile_count)


def pair_total(left_set, right_set, widest):
    flat_left = left_set.reshape(left_set.shape[0], -1)
    flat_right = right_set.reshape(right_set.shape[0], -1)
    total_columns = flat_left.shape[1]
    block_span = math.gcd(total_columns, widest)

    def block_pairs(first_column):
        left_cols = lax.dynamic_slice_in_dim(flat_left, first_column, block_span, 1)
        right_cols = lax.dynamic_slice_in_dim(flat_right, first_column, block_span, 1)
        return jnp.sum(jnp.abs(left_cols[:, None, :] - right_cols[None, :, :]), axis=(0, 1))

    column_starts = jnp.arange(total_columns // block_span, dtype=jnp.int32) * block_span
    return lax.map(block_pairs, column_starts).reshape(left_set.shape[1:])


def reference(ensemble, observed, tile_weight, tile_block, tile_target, tile_count):
    members = ensemble.shape[0]
    channels = members * LEV
    block_count = SRC_DEV // BLOCK
    values = ensemble.reshape(channels, PARTITIONS, block_count, BLOCK)
    values = jnp.moveaxis(values, 1, 0)
    weights = tile_weight.reshape(PARTITIONS, TILES_DEV, BLOCK, BLOCK)
    blocks = tile_block.reshape(PARTITIONS, TILES_DEV)
    targets = tile_target.reshape(PARTITIONS, TILES_DEV)
    slot_index = jnp.arange(TILES_DEV, dtype=jnp.int32)

    def add_partition(summed, inputs):
        part_values, part_weights, part_blocks, part_targets, part_count = inputs
        picked = jnp.take(part_values, part_blocks.astype(jnp.int32), axis=1).astype(jnp.float32)
        partial_value = jnp.einsum('csi,sij->scj', picked, part_weights.astype(jnp.float32), precision=lax.Precision.HIGHEST)
        is_live = (slot_index < part_count).astype(jnp.float32)
        partial_value = partial_value * is_live[:, None, None]
        return summed.at[part_targets.astype(jnp.int32)].add(partial_value), None

    initial = jnp.zeros((PARTITIONS * TGT_DEV // BLOCK, channels, BLOCK), jnp.float32)
    summed, ignored = lax.scan(add_partition, initial, (values, weights, blocks, targets, tile_count))
    tile_total = PARTITIONS * TGT_DEV // BLOCK
    remapped = summed.reshape(tile_total, members, LEV, BLOCK).transpose(1, 2, 0, 3).reshape(members, LEV, tile_total * BLOCK)
    skill_sum = jnp.sum(jnp.abs(remapped - observed[None]), axis=0)
    spread = pair_total(remapped, remapped, 16384)
    return skill_sum / members - spread / (2.0 * members * (members - 1))
```

```python
import functools
import math

import jax
import jax.numpy as jnp
from jax import lax
from jax.experimental import pallas as pl
from jax.experimental.pallas import tpu as pltpu
from jax.sharding import PartitionSpec as P

REACH = 4
PAIR = 2
HALF = REACH // PAIR
UNROLL = 8
MESH = pl.DeviceIdType.MESH


def partial_kernel(unroll, row_ref, block_ref, values_ref, weight_ref, acc_ref):
    step = pl.program_id(0)
    cells = weight_ref.shape[1]

    @pl.when(step == 0)
    def _():
        def clear(row, carry):
            acc_ref[row] = jnp.zeros(acc_ref.shape[1:], jnp.float32)
            return carry

        lax.fori_loop(0, acc_ref.shape[0], clear, 0)

    products = []
    for slot in range(unroll):
        start = pl.multiple_of(block_ref[step * unroll + slot] * cells, cells)
        products.append(
            jnp.dot(
                values_ref[:, pl.ds(start, cells)],
                weight_ref[slot],
                preferred_element_type=jnp.float32,
            )
        )
    for slot in range(unroll):
        acc_ref[row_ref[step * unroll + slot]] += products[slot]


def score_kernel(
    owned, levels, grain, dom_size, mem_size,
    parts_ref, observed_ref, out_ref,
    mine, sib, far, peers, score,
    load_sem, pair_send, pair_recv, far_send, far_recv,
    peer_send, peer_recv, score_send, score_recv,
):
    me = lax.axis_index("dom")
    group = lax.axis_index("mem")
    core = lax.rem(me, PAIR)
    sibling = me + 1 - 2 * core
    share = owned // mem_size
    steps = owned // grain
    share_steps = share // grain
    offsets = [d for k in range(HALF, 0, -1) for d in (k, -k)] + [0]
    chip = lax.div(me, PAIR)
    chips = dom_size // PAIR

    def inside(d):
        return jnp.logical_and(chip + d >= 0, chip + d < chips)

    def tile_at(s):
        return lax.rem((group + 1) * share + s * grain, owned)

    def peer_at(j):
        return lax.rem(group + 1 + j, mem_size)

    def pair_sends(d):
        ok = inside(d)
        if d == HALF:
            ok = jnp.logical_and(ok, core == 1)
        if d == -HALF:
            ok = jnp.logical_and(ok, core == 0)
        return ok

    def pair_gets(d):
        ok = inside(d)
        if d == HALF:
            ok = jnp.logical_and(ok, core == 0)
        if d == -HALF:
            ok = jnp.logical_and(ok, core == 1)
        return ok

    def load(k, d, s):
        row = (PAIR * (d + HALF) + core) * owned + tile_at(s)
        return pltpu.make_async_copy(
            parts_ref.at[pl.ds(row, grain)], mine.at[k, s], load_sem.at[k, s]
        )

    def pair_copy(k, d, s):
        row = (PAIR * (d + HALF) + 1 - core) * owned + tile_at(s)
        return pltpu.make_async_remote_copy(
            src_ref=parts_ref.at[pl.ds(row, grain)],
            dst_ref=sib.at[k, s],
            send_sem=pair_send.at[k, s],
            recv_sem=pair_recv.at[k, s],
            device_id={"dom": sibling},
            device_id_type=MESH,
        )

    def far_copy(k, s, target):
        return pltpu.make_async_remote_copy(
            src_ref=mine.at[k, s],
            dst_ref=far.at[k, s],
            send_sem=far_send.at[k, s],
            recv_sem=far_recv.at[k, s],
            device_id={"dom": target},
            device_id_type=MESH,
        )

    own = len(offsets) - 1

    def peer_copy(s):
        j = lax.div(s, share_steps)
        return pltpu.make_async_remote_copy(
            src_ref=mine.at[own, s],
            dst_ref=peers.at[s],
            send_sem=peer_send.at[s],
            recv_sem=peer_recv.at[s],
            device_id={"mem": peer_at(j)},
            device_id_type=MESH,
        )

    def score_copy(j):
        return pltpu.make_async_remote_copy(
            src_ref=score.at[group],
            dst_ref=score.at[group],
            send_sem=score_send.at[j],
            recv_sem=score_recv.at[j],
            device_id={"mem": peer_at(j)},
            device_id_type=MESH,
        )

    def each_step(body):
        def run(s, carry):
            body(s)
            return carry

        lax.fori_loop(0, steps, run, 0)

    barrier = pltpu.get_barrier_semaphore()
    greeted = jnp.int32(mem_size)
    pl.semaphore_signal(barrier, inc=1, device_id={"dom": sibling}, device_id_type=MESH)
    for j in range(mem_size - 1):
        pl.semaphore_signal(barrier, inc=1, device_id={"mem": peer_at(j)}, device_id_type=MESH)
    for d in offsets[:-1]:
        @pl.when(inside(d))
        def _():
            pl.semaphore_signal(
                barrier, inc=1, device_id={"dom": me + PAIR * d}, device_id_type=MESH
            )

        greeted = greeted + inside(d).astype(jnp.int32)

    @each_step
    def _(s):
        for k, d in enumerate(offsets):
            @pl.when(inside(d))
            def _():
                load(k, d, s).start()

    pl.semaphore_wait(barrier, greeted)

    @each_step
    def _(s):
        for k, d in enumerate(offsets):
            @pl.when(pair_sends(d))
            def _():
                pair_copy(k, d, s).start()

    @each_step
    def _(s):
        for k, d in enumerate(offsets):
            @pl.when(inside(d))
            def _():
                load(k, d, s).wait()

                @pl.when(pair_gets(d))
                def _():
                    pair_copy(k, d, s).wait_recv()
                    mine[k, s] += sib[k, s]

                if d != 0:
                    far_copy(k, s, me + PAIR * d).start()

    @each_step
    def _(s):
        for k, d in enumerate(offsets[:-1]):
            @pl.when(inside(-d))
            def _():
                far_copy(k, s, sibling).wait_recv()
                mine[own, s] += far[k, s]

        if mem_size > 1:
            @pl.when(s < steps - share_steps)
            def _():
                peer_copy(s).start()

    if mem_size > 1:
        def take(s, carry):
            peer_copy(s).wait_recv()
            return carry

        lax.fori_loop(0, steps - share_steps, take, 0)

    groups = mine.shape[3] // levels
    members = groups * mem_size
    rows = 8
    cells = mine.shape[4]
    chunks = levels // rows
    first = steps - share_steps

    def score_chunk(index, carry):
        t = lax.div(index, chunks)
        low = pl.multiple_of(lax.rem(index, chunks) * rows, rows)
        part, place = lax.div(t, grain), lax.rem(t, grain)
        fields = []
        for g in range(groups):
            at = pl.ds(low + g * levels, rows)
            fields.append(mine[own, first + part, place, at, :])
            for j in range(mem_size - 1):
                fields.append(peers[j * share_steps + part, place, at, :])
        seen = observed_ref[
            pl.ds(low, rows), pl.ds(pl.multiple_of((group * share + t) * cells, cells), cells)
        ]
        skill = jnp.abs(fields[0] - seen)
        for field in fields[1:]:
            skill = skill + jnp.abs(field - seen)
        spread = jnp.zeros_like(skill)
        for a in range(members):
            for b in range(a):
                spread = spread + jnp.abs(fields[a] - fields[b])
        score[group, pl.ds(low, rows), pl.ds(pl.multiple_of(t * cells, cells), cells)] = (
            skill / members - spread / (1.0 * members * (members - 1))
        )
        return carry

    lax.fori_loop(0, share * chunks, score_chunk, 0)
    for j in range(mem_size - 1):
        score_copy(j).start()
    for j in range(mem_size - 1):
        score_copy(j).wait_recv()
    for g in range(mem_size):
        out_ref[:, g * share * cells:(g + 1) * share * cells] = score[g]
    for j in range(mem_size - 1):
        score_copy(j).wait_send()

    @each_step
    def _(s):
        for k, d in enumerate(offsets):
            @pl.when(pair_sends(d))
            def _():
                pair_copy(k, d, s).wait_send()

            if d != 0:
                @pl.when(inside(d))
                def _():
                    far_copy(k, s, me + PAIR * d).wait_send()

        if mem_size > 1:
            @pl.when(s < steps - share_steps)
            def _():
                peer_copy(s).wait_send()


def on_device(dom_size, mem_size, ensemble, observed, tile_weight, tile_block, tile_target, tile_count):
    groups, levels, src_cells = ensemble.shape
    cells = tile_weight.shape[1]
    channels = groups * levels
    slots = tile_block.shape[0]
    owned = observed.shape[1] // cells
    window = (2 * REACH + PAIR) * owned
    me = lax.axis_index("dom")
    base = (me - lax.rem(me, PAIR) - REACH) * owned
    is_live = jnp.arange(slots, dtype=jnp.int32) < tile_count[0]
    row = jnp.where(is_live, tile_target - base, window)
    unroll = math.gcd(slots, UNROLL)
    values = ensemble.reshape(channels, src_cells)
    smem = pl.BlockSpec(memory_space=pltpu.SMEM)
    parts = pl.pallas_call(
        functools.partial(partial_kernel, unroll),
        out_shape=jax.ShapeDtypeStruct((window + 1, channels, cells), jnp.float32),
        grid=(slots // unroll,),
        in_specs=[
            smem,
            smem,
            pl.BlockSpec((channels, src_cells), lambda s: (0, 0)),
            pl.BlockSpec((unroll, cells, cells), lambda s: (s, 0, 0)),
        ],
        out_specs=pl.BlockSpec((window + 1, channels, cells), lambda s: (0, 0, 0)),
        compiler_params=pltpu.CompilerParams(vmem_limit_bytes=40 * 2**20),
    )(row, tile_block, values, tile_weight)

    share = owned // mem_size
    grain = math.gcd(share, 2)
    steps = owned // grain
    reach = 2 * HALF + 1
    dma = pltpu.SemaphoreType.DMA
    others = max(mem_size - 1, 1)
    tile = (channels, cells)
    return pl.pallas_call(
        functools.partial(score_kernel, owned, levels, grain, dom_size, mem_size),
        out_shape=jax.ShapeDtypeStruct(observed.shape, jnp.float32),
        in_specs=[
            pl.BlockSpec(memory_space=pl.ANY),
            pl.BlockSpec(memory_space=pltpu.VMEM),
        ],
        out_specs=pl.BlockSpec(memory_space=pltpu.VMEM),
        scratch_shapes=[
            pltpu.VMEM((reach, steps, grain) + tile, jnp.float32),
            pltpu.VMEM((reach, steps, grain) + tile, jnp.float32),
            pltpu.VMEM((reach - 1, steps, grain) + tile, jnp.float32),
            pltpu.VMEM((steps, grain) + tile, jnp.float32),
            pltpu.VMEM((mem_size, levels, share * cells), jnp.float32),
            dma((reach, steps)),
            dma((reach, steps)),
            dma((reach, steps)),
            dma((reach - 1, steps)),
            dma((reach - 1, steps)),
            dma((steps,)),
            dma((steps,)),
            dma((others,)),
            dma((others,)),
        ],
        compiler_params=pltpu.CompilerParams(
            collective_id=0, has_side_effects=True, vmem_limit_bytes=40 * 2**20
        ),
    )(parts, observed)


def solution(mesh):
    return jax.shard_map(
        functools.partial(on_device, mesh.shape["dom"], mesh.shape["mem"]),
        mesh=mesh,
        in_specs=(
            P("mem", None, "dom"),
            P(None, "dom"),
            P("dom", None, None),
            P("dom"),
            P("dom"),
            P("dom"),
        ),
        out_specs=P(None, "dom"),
        check_vma=False,
    )
```

```python
import functools
import math

import jax
import jax.numpy as jnp
from jax import lax
from jax.experimental import pallas as pl
from jax.experimental.pallas import tpu as pltpu
from jax.sharding import PartitionSpec as P

REACH = 4
PAIR = 2
HALF = REACH // PAIR
UNROLL = 8
AHEAD = (1, 2, -1, -2, 0)
MESH = pl.DeviceIdType.MESH


def partial_kernel(
    unroll, owned,
    target_ref, block_ref, count_ref, values_ref, weight_ref, acc_ref,
    targets, blocks, count, values, weights, small_sem, values_sem, weight_sem,
):
    slots, cells = weight_ref.shape[:2]
    window = acc_ref.shape[0] - 1
    me = lax.axis_index("dom")
    base = (me - lax.rem(me, PAIR) - REACH) * owned
    load_values = pltpu.make_async_copy(values_ref, values, values_sem)
    small = [
        pltpu.make_async_copy(block_ref, blocks, small_sem.at[0]),
        pltpu.make_async_copy(target_ref, targets, small_sem.at[1]),
        pltpu.make_async_copy(count_ref, count, small_sem.at[2]),
    ]

    def load_weights(step):
        part = pl.ds(step * unroll, unroll)
        return pltpu.make_async_copy(weight_ref.at[part], weights.at[part], weight_sem.at[step])

    for copy in small:
        copy.start()
    load_values.start()
    for step in range(slots // unroll):
        load_weights(step).start()

    def clear(row, carry):
        acc_ref[row] = jnp.zeros(acc_ref.shape[1:], jnp.float32)
        return carry

    lax.fori_loop(0, window, clear, 0)
    for copy in small:
        copy.wait()
    load_values.wait()

    def add(step, carry):
        load_weights(step).wait()
        products = []
        for k in range(unroll):
            slot = step * unroll + k
            start = pl.multiple_of(blocks[slot] * cells, cells)
            products.append(
                jnp.dot(
                    values[:, pl.ds(start, cells)],
                    weights[slot],
                    preferred_element_type=jnp.float32,
                )
            )
        for k in range(unroll):
            slot = step * unroll + k
            row = jnp.where(slot < count[0], targets[slot] - base, window)
            acc_ref[row] += products[k]
        return carry

    lax.fori_loop(0, slots // unroll, add, 0)


def score_kernel(
    owned, levels, dom_size, mem_size,
    parts_ref, observed_ref, out_ref,
    mine, sib, far, relay, peers, score,
    pair_send, pair_recv, far_send, far_recv, relay_send, relay_recv,
    peer_send, peer_recv, score_send, score_recv,
):
    me = lax.axis_index("dom")
    group = lax.axis_index("mem")
    core = lax.rem(me, PAIR)
    sibling = me + 1 - 2 * core
    share = owned // mem_size
    first = owned - share
    chip = lax.div(me, PAIR)
    chips = dom_size // PAIR
    way = 2 * lax.rem(chip, 2) - 1
    own = len(AHEAD) - 1

    def inside(ahead):
        there = chip + ahead * way
        return jnp.logical_and(there >= 0, there < chips)

    def device_at(ahead):
        return me + PAIR * ahead * way

    def tile_at(s):
        return lax.rem((group + 1) * share + s, owned)

    def peer_at(j):
        return lax.rem(group + 1 + j, mem_size)

    def row_of(k, which, s):
        return (PAIR * (AHEAD[k] * way + HALF) + which) * owned + tile_at(s)

    def reaches(k, which):
        d = AHEAD[k] * way
        over = jnp.logical_and(d == HALF, which == 1)
        under = jnp.logical_and(d == -HALF, which == 0)
        return jnp.logical_and(
            inside(AHEAD[k]), jnp.logical_not(jnp.logical_or(over, under))
        )

    def pair_copy(k, s):
        return pltpu.make_async_remote_copy(
            src_ref=parts_ref.at[row_of(k, 1 - core, s)],
            dst_ref=sib.at[k, s],
            send_sem=pair_send.at[k, s],
            recv_sem=pair_recv.at[k, s],
            device_id={"dom": sibling},
            device_id_type=MESH,
        )

    def far_copy(k, s):
        return pltpu.make_async_remote_copy(
            src_ref=mine.at[k, s],
            dst_ref=far.at[k - 1, s],
            send_sem=far_send.at[k - 1, s],
            recv_sem=far_recv.at[k - 1, s],
            device_id={"dom": device_at(AHEAD[k])},
            device_id_type=MESH,
        )

    def relay_copy(s):
        ahead = 2 - 3 * lax.rem(s, 2)
        return pltpu.make_async_remote_copy(
            src_ref=mine.at[0, s],
            dst_ref=relay.at[s],
            send_sem=relay_send.at[s],
            recv_sem=relay_recv.at[s],
            device_id={"dom": device_at(ahead)},
            device_id_type=MESH,
        )

    def peer_copy(s):
        return pltpu.make_async_remote_copy(
            src_ref=mine.at[own, s],
            dst_ref=peers.at[s],
            send_sem=peer_send.at[s],
            recv_sem=peer_recv.at[s],
            device_id={"mem": peer_at(lax.div(s, share))},
            device_id_type=MESH,
        )

    def score_copy(j, t):
        return pltpu.make_async_remote_copy(
            src_ref=score.at[group, t],
            dst_ref=score.at[group, t],
            send_sem=score_send.at[j, t],
            recv_sem=score_recv.at[j, t],
            device_id={"mem": peer_at(j)},
            device_id_type=MESH,
        )

    def each(start, stop, body):
        def run(s, carry):
            body(s)
            return carry

        lax.fori_loop(start, stop, run, 0)

    def gather_pair(k, s):
        @pl.when(reaches(k, core))
        def _():
            pair_copy(k, s).wait_recv()
            mine[k, s] = parts_ref[row_of(k, core, s)] + sib[k, s]

        @pl.when(jnp.logical_not(reaches(k, core)))
        def _():
            mine[k, s] = parts_ref[row_of(k, core, s)]

    barrier = pltpu.get_barrier_semaphore()
    greeted = jnp.int32(mem_size + 1)
    pl.semaphore_signal(barrier, inc=1, device_id={"dom": sibling}, device_id_type=MESH)
    pl.semaphore_signal(barrier, inc=1, device_id={"dom": device_at(-1)}, device_id_type=MESH)
    for j in range(mem_size - 1):
        pl.semaphore_signal(barrier, inc=1, device_id={"mem": peer_at(j)}, device_id_type=MESH)
    for ahead in (2, -2):
        @pl.when(inside(ahead))
        def _():
            pl.semaphore_signal(
                barrier, inc=1, device_id={"dom": device_at(ahead)}, device_id_type=MESH
            )

        greeted = greeted + inside(ahead).astype(jnp.int32)
    pl.semaphore_wait(barrier, greeted)

    def start_pair(k, s):
        @pl.when(reaches(k, 1 - core))
        def _():
            pair_copy(k, s).start()

    @functools.partial(each, 0, owned)
    def _(s):
        start_pair(0, s)

    @functools.partial(each, 0, owned)
    def _(s):
        for k in range(1, own + 1):
            start_pair(k, s)

    @functools.partial(each, 0, owned)
    def _(s):
        @pl.when(inside(2))
        def _():
            gather_pair(0, s)
            relay_copy(s).start()

    @functools.partial(each, 0, owned)
    def _(s):
        even = lax.rem(s, 2) == 0

        @pl.when(inside(2))
        def _():
            gather_pair(1, s)
            far_copy(1, s).start()

        gather_pair(2, s)

        @pl.when(jnp.logical_not(jnp.logical_and(even, inside(-2))))
        def _():
            far_copy(2, s).start()

        @pl.when(inside(-2))
        def _():
            gather_pair(3, s)

            @pl.when(even)
            def _():
                far_copy(3, s).start()

            relay_copy(s).wait_recv()

            @pl.when(even)
            def _():
                mine[2, s] += relay[s]
                far_copy(2, s).start()

            @pl.when(jnp.logical_not(even))
            def _():
                mine[3, s] += relay[s]
                far_copy(3, s).start()

        gather_pair(own, s)

    def total(s):
        far_copy(2, s).wait_recv()
        mine[own, s] += far[1, s]

        @pl.when(inside(-2))
        def _():
            far_copy(1, s).wait_recv()
            mine[own, s] += far[0, s]

        @pl.when(inside(2))
        def _():
            far_copy(3, s).wait_recv()
            mine[own, s] += far[2, s]

    @functools.partial(each, 0, first)
    def _(s):
        total(s)
        peer_copy(s).start()

    groups = mine.shape[2] // levels
    members = groups * mem_size
    rows = 8
    cells = mine.shape[3]

    @functools.partial(each, 0, share)
    def _(t):
        total(first + t)
        for j in range(mem_size - 1):
            peer_copy(j * share + t).wait_recv()
        column = pl.ds(pl.multiple_of((group * share + t) * cells, cells), cells)

        def score_rows(chunk, carry):
            low = pl.multiple_of(chunk * rows, rows)
            fields = []
            for g in range(groups):
                at = pl.ds(low + g * levels, rows)
                fields.append(mine[own, first + t, at, :])
                for j in range(mem_size - 1):
                    fields.append(peers[j * share + t, at, :])
            seen = observed_ref[pl.ds(low, rows), column]
            skill = jnp.abs(fields[0] - seen)
            for field in fields[1:]:
                skill = skill + jnp.abs(field - seen)
            spread = jnp.zeros_like(skill)
            for a in range(members):
                for b in range(a):
                    spread = spread + jnp.abs(fields[a] - fields[b])
            score[group, t, pl.ds(low, rows), :] = (
                skill / members - spread / (1.0 * members * (members - 1))
            )
            return carry

        lax.fori_loop(0, levels // rows, score_rows, 0)
        for j in range(mem_size - 1):
            score_copy(j, t).start()

    for t in range(share):
        for j in range(mem_size - 1):
            score_copy(j, t).wait_recv()
    for g in range(mem_size):
        for t in range(share):
            at = (g * share + t) * cells
            out_ref[:, at:at + cells] = score[g, t]
    for t in range(share):
        for j in range(mem_size - 1):
            score_copy(j, t).wait_send()

    @functools.partial(each, 0, owned)
    def _(s):
        for k in range(own + 1):
            @pl.when(reaches(k, 1 - core))
            def _():
                pair_copy(k, s).wait_send()

        far_copy(2, s).wait_send()

        @pl.when(inside(2))
        def _():
            relay_copy(s).wait_send()
            far_copy(1, s).wait_send()

        @pl.when(inside(-2))
        def _():
            far_copy(3, s).wait_send()

        @pl.when(s < first)
        def _():
            peer_copy(s).wait_send()


def on_device(dom_size, mem_size, ensemble, observed, tile_weight, tile_block, tile_target, tile_count):
    groups, levels, src_cells = ensemble.shape
    cells = tile_weight.shape[1]
    channels = groups * levels
    slots = tile_block.shape[0]
    owned = observed.shape[1] // cells
    window = (2 * REACH + PAIR) * owned
    unroll = math.gcd(slots, UNROLL)
    values = ensemble.reshape(channels, src_cells)
    dma = pltpu.SemaphoreType.DMA
    hbm = pl.BlockSpec(memory_space=pltpu.HBM)
    vmem = pl.BlockSpec(memory_space=pltpu.VMEM)
    parts = pl.pallas_call(
        functools.partial(partial_kernel, unroll, owned),
        out_shape=jax.ShapeDtypeStruct((window + 1, channels, cells), jnp.float32),
        in_specs=[hbm] * 5,
        out_specs=vmem,
        scratch_shapes=[
            pltpu.SMEM((slots,), jnp.int32),
            pltpu.SMEM((slots,), jnp.int32),
            pltpu.SMEM((1,), jnp.int32),
            pltpu.VMEM(values.shape, values.dtype),
            pltpu.VMEM(tile_weight.shape, tile_weight.dtype),
            dma((3,)),
            dma,
            dma((slots // unroll,)),
        ],
        compiler_params=pltpu.CompilerParams(vmem_limit_bytes=28 * 2**20),
    )(tile_target, tile_block, tile_count, values, tile_weight)

    share = owned // mem_size
    kinds = len(AHEAD)
    others = max(mem_size - 1, 1)
    tile = (channels, cells)
    return pl.pallas_call(
        functools.partial(score_kernel, owned, levels, dom_size, mem_size),
        out_shape=jax.ShapeDtypeStruct(observed.shape, jnp.float32),
        in_specs=[vmem, vmem],
        out_specs=vmem,
        scratch_shapes=[
            pltpu.VMEM((kinds, owned) + tile, jnp.float32),
            pltpu.VMEM((kinds, owned) + tile, jnp.float32),
            pltpu.VMEM((kinds - 2, owned) + tile, jnp.float32),
            pltpu.VMEM((owned,) + tile, jnp.float32),
            pltpu.VMEM((owned,) + tile, jnp.float32),
            pltpu.VMEM((mem_size, share, levels, cells), jnp.float32),
            dma((kinds, owned)),
            dma((kinds, owned)),
            dma((kinds - 2, owned)),
            dma((kinds - 2, owned)),
            dma((owned,)),
            dma((owned,)),
            dma((owned,)),
            dma((owned,)),
            dma((others, share)),
            dma((others, share)),
        ],
        compiler_params=pltpu.CompilerParams(
            collective_id=0, has_side_effects=True, vmem_limit_bytes=36 * 2**20
        ),
    )(parts, observed)


def solution(mesh):
    return jax.shard_map(
        functools.partial(on_device, mesh.shape["dom"], mesh.shape["mem"]),
        mesh=mesh,
        in_specs=(
            P("mem", None, "dom"),
            P(None, "dom"),
            P("dom", None, None),
            P("dom"),
            P("dom"),
            P("dom"),
        ),
        out_specs=P(None, "dom"),
        check_vma=False,
    )
```

```python
import functools
import math

import jax
import jax.numpy as jnp
from jax import lax
from jax.experimental import pallas as pl
from jax.experimental.pallas import tpu as pltpu
from jax.sharding import PartitionSpec as P

REACH = 4
PAIR = 2
HALF = REACH // PAIR
UNROLL = 32
AHEAD = (1, 2, -1, -2, 0)
MESH = pl.DeviceIdType.MESH


def partial_kernel(
    unroll, shift,
    packed, values, weights, acc_ref,
):
    slots, cells = weights.shape[:2]
    window = acc_ref.shape[0] - 1

    def clear(row, carry):
        acc_ref[row] = jnp.zeros(acc_ref.shape[1:], jnp.float32)
        return carry

    lax.fori_loop(0, window, clear, 0)
    def add(step, carry):
        products = []
        for k in range(unroll):
            slot = step * unroll + k
            start = pl.multiple_of((packed[slot] & ((1 << shift) - 1)) * cells, cells)
            products.append(
                jnp.dot(
                    values[:, pl.ds(start, cells)],
                    weights[slot],
                    preferred_element_type=jnp.float32,
                )
            )
        for k in range(unroll):
            slot = step * unroll + k
            acc_ref[packed[slot] >> shift] += products[k]
        return carry

    lax.fori_loop(0, slots // unroll, add, 0)


def score_kernel(
    owned, levels, dom_size, mem_size,
    parts_ref, observed_ref, out_ref,
    mine, sib, far, relay, peers, score,
    pair_send, pair_recv, far_send, far_recv, relay_send, relay_recv,
    peer_send, peer_recv, score_send, score_recv,
):
    me = lax.axis_index("dom")
    group = lax.axis_index("mem")
    core = lax.rem(me, PAIR)
    sibling = me + 1 - 2 * core
    share = owned // mem_size
    first = owned - share
    chip = lax.div(me, PAIR)
    chips = dom_size // PAIR
    way = 2 * lax.rem(chip, 2) - 1
    own = len(AHEAD) - 1

    def inside(ahead):
        there = chip + ahead * way
        return jnp.logical_and(there >= 0, there < chips)

    def device_at(ahead):
        return me + PAIR * ahead * way

    def tile_at(s):
        return lax.rem((group + 1) * share + s, owned)

    def peer_at(j):
        return lax.rem(group + 1 + j, mem_size)

    def row_of(k, which, s):
        return (PAIR * (AHEAD[k] * way + HALF) + which) * owned + tile_at(s)

    def reaches(k, which):
        d = AHEAD[k] * way
        over = jnp.logical_and(d == HALF, which == 1)
        under = jnp.logical_and(d == -HALF, which == 0)
        return jnp.logical_and(
            inside(AHEAD[k]), jnp.logical_not(jnp.logical_or(over, under))
        )

    def pair_copy(k, s):
        return pltpu.make_async_remote_copy(
            src_ref=parts_ref.at[row_of(k, 1 - core, s)],
            dst_ref=sib.at[k, s],
            send_sem=pair_send.at[k, s],
            recv_sem=pair_recv.at[k, s],
            device_id={"dom": sibling},
            device_id_type=MESH,
        )

    def far_copy(k, s):
        return pltpu.make_async_remote_copy(
            src_ref=mine.at[k, s],
            dst_ref=far.at[k - 1, s],
            send_sem=far_send.at[k - 1, s],
            recv_sem=far_recv.at[k - 1, s],
            device_id={"dom": device_at(AHEAD[k])},
            device_id_type=MESH,
        )

    def relay_copy(s):
        ahead = 2 - 3 * lax.rem(s, 2)
        return pltpu.make_async_remote_copy(
            src_ref=mine.at[0, s],
            dst_ref=relay.at[s],
            send_sem=relay_send.at[s],
            recv_sem=relay_recv.at[s],
            device_id={"dom": device_at(ahead)},
            device_id_type=MESH,
        )

    def peer_copy(s):
        return pltpu.make_async_remote_copy(
            src_ref=mine.at[own, s],
            dst_ref=peers.at[s],
            send_sem=peer_send.at[s],
            recv_sem=peer_recv.at[s],
            device_id={"mem": peer_at(lax.div(s, share))},
            device_id_type=MESH,
        )

    def score_copy(j, t):
        return pltpu.make_async_remote_copy(
            src_ref=score.at[group, t],
            dst_ref=score.at[group, t],
            send_sem=score_send.at[j, t],
            recv_sem=score_recv.at[j, t],
            device_id={"mem": peer_at(j)},
            device_id_type=MESH,
        )

    def each(start, stop, body):
        def run(s, carry):
            body(s)
            return carry

        lax.fori_loop(start, stop, run, 0)

    def gather_pair(k, s):
        @pl.when(reaches(k, core))
        def _():
            pair_copy(k, s).wait_recv()
            mine[k, s] = parts_ref[row_of(k, core, s)] + sib[k, s]

        @pl.when(jnp.logical_not(reaches(k, core)))
        def _():
            mine[k, s] = parts_ref[row_of(k, core, s)]

    barrier = pltpu.get_barrier_semaphore()
    greeted = jnp.int32(mem_size + 1)
    pl.semaphore_signal(barrier, inc=1, device_id={"dom": sibling}, device_id_type=MESH)
    pl.semaphore_signal(barrier, inc=1, device_id={"dom": device_at(-1)}, device_id_type=MESH)
    for j in range(mem_size - 1):
        pl.semaphore_signal(barrier, inc=1, device_id={"mem": peer_at(j)}, device_id_type=MESH)
    for ahead in (2, -2):
        @pl.when(inside(ahead))
        def _():
            pl.semaphore_signal(
                barrier, inc=1, device_id={"dom": device_at(ahead)}, device_id_type=MESH
            )

        greeted = greeted + inside(ahead).astype(jnp.int32)
    pl.semaphore_wait(barrier, greeted)

    def start_pair(k, s):
        @pl.when(reaches(k, 1 - core))
        def _():
            pair_copy(k, s).start()

    @functools.partial(each, 0, owned)
    def _(s):
        start_pair(0, s)

    @functools.partial(each, 0, owned)
    def _(s):
        for k in range(1, own + 1):
            start_pair(k, s)

    @functools.partial(each, 0, owned)
    def _(s):
        @pl.when(inside(2))
        def _():
            gather_pair(0, s)
            relay_copy(s).start()

    @functools.partial(each, 0, owned)
    def _(s):
        even = lax.rem(s, 2) == 0

        @pl.when(inside(2))
        def _():
            gather_pair(1, s)
            far_copy(1, s).start()

        gather_pair(2, s)

        @pl.when(jnp.logical_not(jnp.logical_and(even, inside(-2))))
        def _():
            far_copy(2, s).start()

        @pl.when(inside(-2))
        def _():
            gather_pair(3, s)

            @pl.when(even)
            def _():
                far_copy(3, s).start()

            relay_copy(s).wait_recv()

            @pl.when(even)
            def _():
                mine[2, s] += relay[s]
                far_copy(2, s).start()

            @pl.when(jnp.logical_not(even))
            def _():
                mine[3, s] += relay[s]
                far_copy(3, s).start()

        gather_pair(own, s)

    def total(s):
        far_copy(2, s).wait_recv()
        mine[own, s] += far[1, s]

        @pl.when(inside(-2))
        def _():
            far_copy(1, s).wait_recv()
            mine[own, s] += far[0, s]

        @pl.when(inside(2))
        def _():
            far_copy(3, s).wait_recv()
            mine[own, s] += far[2, s]

    @functools.partial(each, 0, first)
    def _(s):
        total(s)
        peer_copy(s).start()

    groups = mine.shape[2] // levels
    members = groups * mem_size
    rows = 8
    cells = mine.shape[3]

    @functools.partial(each, 0, share)
    def _(t):
        total(first + t)
        for j in range(mem_size - 1):
            peer_copy(j * share + t).wait_recv()
        column = pl.ds(pl.multiple_of((group * share + t) * cells, cells), cells)

        def score_rows(chunk, carry):
            low = pl.multiple_of(chunk * rows, rows)
            fields = []
            for g in range(groups):
                at = pl.ds(low + g * levels, rows)
                fields.append(mine[own, first + t, at, :])
                for j in range(mem_size - 1):
                    fields.append(peers[j * share + t, at, :])
            seen = observed_ref[pl.ds(low, rows), column]
            skill = jnp.abs(fields[0] - seen)
            for field in fields[1:]:
                skill = skill + jnp.abs(field - seen)
            spread = jnp.zeros_like(skill)
            for a in range(members):
                for b in range(a):
                    spread = spread + jnp.abs(fields[a] - fields[b])
            score[group, t, pl.ds(low, rows), :] = (
                skill / members - spread / (1.0 * members * (members - 1))
            )
            return carry

        lax.fori_loop(0, levels // rows, score_rows, 0)
        for j in range(mem_size - 1):
            score_copy(j, t).start()

    for t in range(share):
        for j in range(mem_size - 1):
            score_copy(j, t).wait_recv()
    for g in range(mem_size):
        for t in range(share):
            at = (g * share + t) * cells
            out_ref[:, at:at + cells] = score[g, t]
    for t in range(share):
        for j in range(mem_size - 1):
            score_copy(j, t).wait_send()

    @functools.partial(each, 0, owned)
    def _(s):
        for k in range(own + 1):
            @pl.when(reaches(k, 1 - core))
            def _():
                pair_copy(k, s).wait_send()

        far_copy(2, s).wait_send()

        @pl.when(inside(2))
        def _():
            relay_copy(s).wait_send()
            far_copy(1, s).wait_send()

        @pl.when(inside(-2))
        def _():
            far_copy(3, s).wait_send()

        @pl.when(s < first)
        def _():
            peer_copy(s).wait_send()


def on_device(dom_size, mem_size, ensemble, observed, tile_weight, tile_block, tile_target, tile_count):
    groups, levels, src_cells = ensemble.shape
    cells = tile_weight.shape[1]
    channels = groups * levels
    slots = tile_block.shape[0]
    owned = observed.shape[1] // cells
    window = (2 * REACH + PAIR) * owned
    unroll = math.gcd(slots, UNROLL)
    me = lax.axis_index("dom")
    base = (me - lax.rem(me, PAIR) - REACH) * owned
    is_live = jnp.arange(slots, dtype=jnp.int32) < tile_count[0]
    shift = (src_cells // cells - 1).bit_length()
    packed = (jnp.where(is_live, tile_target - base, window) << shift) + tile_block
    values = ensemble.reshape(channels, src_cells)
    dma = pltpu.SemaphoreType.DMA
    smem = pl.BlockSpec(memory_space=pltpu.SMEM)
    vmem = pl.BlockSpec(memory_space=pltpu.VMEM)
    parts = pl.pallas_call(
        functools.partial(partial_kernel, unroll, shift),
        out_shape=jax.ShapeDtypeStruct((window + 1, channels, cells), jnp.float32),
        in_specs=[smem] + [vmem] * 2,
        out_specs=vmem,
        compiler_params=pltpu.CompilerParams(vmem_limit_bytes=28 * 2**20),
    )(packed, values, tile_weight)

    share = owned // mem_size
    kinds = len(AHEAD)
    others = max(mem_size - 1, 1)
    tile = (channels, cells)
    return pl.pallas_call(
        functools.partial(score_kernel, owned, levels, dom_size, mem_size),
        out_shape=jax.ShapeDtypeStruct(observed.shape, jnp.float32),
        in_specs=[vmem, vmem],
        out_specs=vmem,
        scratch_shapes=[
            pltpu.VMEM((kinds, owned) + tile, jnp.float32),
            pltpu.VMEM((kinds, owned) + tile, jnp.float32),
            pltpu.VMEM((kinds - 2, owned) + tile, jnp.float32),
            pltpu.VMEM((owned,) + tile, jnp.float32),
            pltpu.VMEM((owned,) + tile, jnp.float32),
            pltpu.VMEM((mem_size, share, levels, cells), jnp.float32),
            dma((kinds, owned)),
            dma((kinds, owned)),
            dma((kinds - 2, owned)),
            dma((kinds - 2, owned)),
            dma((owned,)),
            dma((owned,)),
            dma((owned,)),
            dma((owned,)),
            dma((others, share)),
            dma((others, share)),
        ],
        compiler_params=pltpu.CompilerParams(
            collective_id=0, has_side_effects=True, vmem_limit_bytes=36 * 2**20
        ),
    )(parts, observed)


def solution(mesh):
    return jax.shard_map(
        functools.partial(on_device, mesh.shape["dom"], mesh.shape["mem"]),
        mesh=mesh,
        in_specs=(
            P("mem", None, "dom"),
            P(None, "dom"),
            P("dom", None, None),
            P("dom"),
            P("dom"),
            P("dom"),
        ),
        out_specs=P(None, "dom"),
        check_vma=False,
    )
```

```python
import functools
import math

import jax
import jax.numpy as jnp
from jax import lax
from jax.experimental import pallas as pl
from jax.experimental.pallas import tpu as pltpu
from jax.sharding import PartitionSpec as P

REACH = 4
PAIR = 2
HALF = REACH // PAIR
UNROLL = 32
AHEAD = (1, 2, -1, -2, 0)
MESH = pl.DeviceIdType.MESH


def partial_kernel(
    unroll, shift,
    packed, values, weights, acc_ref,
):
    slots, cells = weights.shape[:2]
    window = acc_ref.shape[0] - 1

    def clear(row, carry):
        acc_ref[row] = jnp.zeros(acc_ref.shape[1:], jnp.float32)
        return carry

    lax.fori_loop(0, window, clear, 0)
    def add(step, carry):
        products = []
        for k in range(unroll):
            slot = step * unroll + k
            start = pl.multiple_of((packed[slot] & ((1 << shift) - 1)) * cells, cells)
            products.append(
                jnp.dot(
                    values[:, pl.ds(start, cells)],
                    weights[slot],
                    preferred_element_type=jnp.float32,
                )
            )
        for k in range(unroll):
            slot = step * unroll + k
            acc_ref[packed[slot] >> shift] += products[k]
        return carry

    lax.fori_loop(0, slots // unroll, add, 0)


def score_kernel(
    owned, levels, dom_size, mem_size,
    parts_ref, observed_ref, out_ref,
    mine, sib, far, relay, peers, score,
    pair_send, pair_recv, far_send, far_recv, relay_send, relay_recv,
    peer_send, peer_recv, score_send, score_recv,
):
    me = lax.axis_index("dom")
    group = lax.axis_index("mem")
    core = lax.rem(me, PAIR)
    sibling = me + 1 - 2 * core
    share = owned // mem_size
    first = owned - share
    chip = lax.div(me, PAIR)
    chips = dom_size // PAIR
    way = 2 * lax.rem(chip, 2) - 1
    own = len(AHEAD) - 1

    def inside(ahead):
        there = chip + ahead * way
        return jnp.logical_and(there >= 0, there < chips)

    def device_at(ahead):
        return me + PAIR * ahead * way

    def tile_at(s):
        return lax.rem((group + 1) * share + s, owned)

    def peer_at(j):
        return lax.rem(group + 1 + j, mem_size)

    def row_of(k, which, s):
        return (PAIR * (AHEAD[k] * way + HALF) + which) * owned + tile_at(s)

    def reaches(k, which):
        d = AHEAD[k] * way
        over = jnp.logical_and(d == HALF, which == 1)
        under = jnp.logical_and(d == -HALF, which == 0)
        return jnp.logical_and(
            inside(AHEAD[k]), jnp.logical_not(jnp.logical_or(over, under))
        )

    def pair_copy(k, s):
        return pltpu.make_async_remote_copy(
            src_ref=parts_ref.at[row_of(k, 1 - core, s)],
            dst_ref=sib.at[k, s],
            send_sem=pair_send.at[k, s],
            recv_sem=pair_recv.at[k, s],
            device_id={"dom": sibling},
            device_id_type=MESH,
        )

    def far_copy(k, s):
        return pltpu.make_async_remote_copy(
            src_ref=mine.at[k, s],
            dst_ref=far.at[k - 1, s],
            send_sem=far_send.at[k - 1, s],
            recv_sem=far_recv.at[k - 1, s],
            device_id={"dom": device_at(AHEAD[k])},
            device_id_type=MESH,
        )

    def relay_copy(s):
        ahead = 2 - 3 * lax.rem(s, 2)
        return pltpu.make_async_remote_copy(
            src_ref=mine.at[0, s],
            dst_ref=relay.at[s],
            send_sem=relay_send.at[s],
            recv_sem=relay_recv.at[s],
            device_id={"dom": device_at(ahead)},
            device_id_type=MESH,
        )

    def peer_copy(s):
        return pltpu.make_async_remote_copy(
            src_ref=mine.at[own, s],
            dst_ref=peers.at[s],
            send_sem=peer_send.at[s],
            recv_sem=peer_recv.at[s],
            device_id={"mem": peer_at(lax.div(s, share))},
            device_id_type=MESH,
        )

    def score_copy(j, t):
        return pltpu.make_async_remote_copy(
            src_ref=score.at[group, t],
            dst_ref=score.at[group, t],
            send_sem=score_send.at[j, t],
            recv_sem=score_recv.at[j, t],
            device_id={"mem": peer_at(j)},
            device_id_type=MESH,
        )

    def each(start, stop, body):
        def run(s, carry):
            body(s)
            return carry

        lax.fori_loop(start, stop, run, 0)

    def gather_pair(k, s):
        @pl.when(reaches(k, core))
        def _():
            pair_copy(k, s).wait_recv()
            mine[k, s] = parts_ref[row_of(k, core, s)] + sib[k, s]

        @pl.when(jnp.logical_not(reaches(k, core)))
        def _():
            mine[k, s] = parts_ref[row_of(k, core, s)]

    barrier = pltpu.get_barrier_semaphore()
    greeted = jnp.int32(mem_size + 1)
    pl.semaphore_signal(barrier, inc=1, device_id={"dom": sibling}, device_id_type=MESH)
    pl.semaphore_signal(barrier, inc=1, device_id={"dom": device_at(-1)}, device_id_type=MESH)
    for j in range(mem_size - 1):
        pl.semaphore_signal(barrier, inc=1, device_id={"mem": peer_at(j)}, device_id_type=MESH)
    for ahead in (2, -2):
        @pl.when(inside(ahead))
        def _():
            pl.semaphore_signal(
                barrier, inc=1, device_id={"dom": device_at(ahead)}, device_id_type=MESH
            )

        greeted = greeted + inside(ahead).astype(jnp.int32)
    pl.semaphore_wait(barrier, greeted)

    def start_pair(k, s):
        @pl.when(reaches(k, 1 - core))
        def _():
            pair_copy(k, s).start()

    @functools.partial(each, 0, owned)
    def _(s):
        start_pair(0, s)

    @functools.partial(each, 0, owned)
    def _(s):
        for k in range(1, own + 1):
            start_pair(k, s)

    @functools.partial(each, 0, owned)
    def _(s):
        @pl.when(inside(2))
        def _():
            gather_pair(0, s)
            relay_copy(s).start()

    @functools.partial(each, 0, owned)
    def _(s):
        even = lax.rem(s, 2) == 0

        gather_pair(2, s)

        @pl.when(jnp.logical_not(jnp.logical_and(even, inside(-2))))
        def _():
            far_copy(2, s).start()

        @pl.when(inside(-2))
        def _():
            gather_pair(3, s)

            @pl.when(even)
            def _():
                far_copy(3, s).start()

            relay_copy(s).wait_recv()

            @pl.when(even)
            def _():
                mine[2, s] += relay[s]
                far_copy(2, s).start()

            @pl.when(jnp.logical_not(even))
            def _():
                mine[3, s] += relay[s]
                far_copy(3, s).start()

        @pl.when(inside(2))
        def _():
            gather_pair(1, s)
            far_copy(1, s).start()

    def total(s):
        gather_pair(own, s)
        far_copy(2, s).wait_recv()
        mine[own, s] += far[1, s]

        @pl.when(inside(-2))
        def _():
            far_copy(1, s).wait_recv()
            mine[own, s] += far[0, s]

        @pl.when(inside(2))
        def _():
            far_copy(3, s).wait_recv()
            mine[own, s] += far[2, s]

    @functools.partial(each, 0, first)
    def _(s):
        total(s)
        peer_copy(s).start()

    groups = mine.shape[2] // levels
    members = groups * mem_size
    rows = 8
    cells = mine.shape[3]

    @functools.partial(each, 0, share)
    def _(t):
        total(first + t)
        for j in range(mem_size - 1):
            peer_copy(j * share + t).wait_recv()
        column = pl.ds(pl.multiple_of((group * share + t) * cells, cells), cells)

        def score_rows(chunk, carry):
            low = pl.multiple_of(chunk * rows, rows)
            fields = []
            for g in range(groups):
                at = pl.ds(low + g * levels, rows)
                fields.append(mine[own, first + t, at, :])
                for j in range(mem_size - 1):
                    fields.append(peers[j * share + t, at, :])
            seen = observed_ref[pl.ds(low, rows), column]
            skill = jnp.abs(fields[0] - seen)
            for field in fields[1:]:
                skill = skill + jnp.abs(field - seen)
            spread = jnp.zeros_like(skill)
            for a in range(members):
                for b in range(a):
                    spread = spread + jnp.abs(fields[a] - fields[b])
            score[group, t, pl.ds(low, rows), :] = (
                skill / members - spread / (1.0 * members * (members - 1))
            )
            return carry

        lax.fori_loop(0, levels // rows, score_rows, 0)
        for j in range(mem_size - 1):
            score_copy(j, t).start()

    for t in range(share):
        for j in range(mem_size - 1):
            score_copy(j, t).wait_recv()
    for g in range(mem_size):
        for t in range(share):
            at = (g * share + t) * cells
            out_ref[:, at:at + cells] = score[g, t]
    for t in range(share):
        for j in range(mem_size - 1):
            score_copy(j, t).wait_send()

    @functools.partial(each, 0, owned)
    def _(s):
        for k in range(own + 1):
            @pl.when(reaches(k, 1 - core))
            def _():
                pair_copy(k, s).wait_send()

        far_copy(2, s).wait_send()

        @pl.when(inside(2))
        def _():
            relay_copy(s).wait_send()
            far_copy(1, s).wait_send()

        @pl.when(inside(-2))
        def _():
            far_copy(3, s).wait_send()

        @pl.when(s < first)
        def _():
            peer_copy(s).wait_send()


def on_device(dom_size, mem_size, ensemble, observed, tile_weight, tile_block, tile_target, tile_count):
    groups, levels, src_cells = ensemble.shape
    cells = tile_weight.shape[1]
    channels = groups * levels
    slots = tile_block.shape[0]
    owned = observed.shape[1] // cells
    window = (2 * REACH + PAIR) * owned
    unroll = math.gcd(slots, UNROLL)
    me = lax.axis_index("dom")
    base = (me - lax.rem(me, PAIR) - REACH) * owned
    is_live = jnp.arange(slots, dtype=jnp.int32) < tile_count[0]
    shift = (src_cells // cells - 1).bit_length()
    packed = (jnp.where(is_live, tile_target - base, window) << shift) + tile_block
    values = ensemble.reshape(channels, src_cells)
    dma = pltpu.SemaphoreType.DMA
    smem = pl.BlockSpec(memory_space=pltpu.SMEM)
    vmem = pl.BlockSpec(memory_space=pltpu.VMEM)
    parts = pl.pallas_call(
        functools.partial(partial_kernel, unroll, shift),
        out_shape=jax.ShapeDtypeStruct((window + 1, channels, cells), jnp.float32),
        in_specs=[smem] + [vmem] * 2,
        out_specs=vmem,
        compiler_params=pltpu.CompilerParams(vmem_limit_bytes=28 * 2**20),
    )(packed, values, tile_weight)

    share = owned // mem_size
    kinds = len(AHEAD)
    others = max(mem_size - 1, 1)
    tile = (channels, cells)
    return pl.pallas_call(
        functools.partial(score_kernel, owned, levels, dom_size, mem_size),
        out_shape=jax.ShapeDtypeStruct(observed.shape, jnp.float32),
        in_specs=[vmem, vmem],
        out_specs=vmem,
        scratch_shapes=[
            pltpu.VMEM((kinds, owned) + tile, jnp.float32),
            pltpu.VMEM((kinds, owned) + tile, jnp.float32),
            pltpu.VMEM((kinds - 2, owned) + tile, jnp.float32),
            pltpu.VMEM((owned,) + tile, jnp.float32),
            pltpu.VMEM((owned,) + tile, jnp.float32),
            pltpu.VMEM((mem_size, share, levels, cells), jnp.float32),
            dma((kinds, owned)),
            dma((kinds, owned)),
            dma((kinds - 2, owned)),
            dma((kinds - 2, owned)),
            dma((owned,)),
            dma((owned,)),
            dma((owned,)),
            dma((owned,)),
            dma((others, share)),
            dma((others, share)),
        ],
        compiler_params=pltpu.CompilerParams(
            collective_id=0, has_side_effects=True, vmem_limit_bytes=36 * 2**20
        ),
    )(parts, observed)


def solution(mesh):
    return jax.shard_map(
        functools.partial(on_device, mesh.shape["dom"], mesh.shape["mem"]),
        mesh=mesh,
        in_specs=(
            P("mem", None, "dom"),
            P(None, "dom"),
            P("dom", None, None),
            P("dom"),
            P("dom"),
            P("dom"),
        ),
        out_specs=P(None, "dom"),
        check_vma=False,
    )
```
